32 devices in a mesh: samp: 2 (over x), cpg: 16 (over z, y, core).
Axes of the slice: x: 2, y: 2, z: 4, core: 2. Of those that a mesh axis runs over, the one named last changes fastest.
Arguments:
- methylation: bfloat16 [512, 114688], P('samp', 'cpg'), may hold values from -6 to 6
- labels: int32 [512], P('samp'), may hold values from 0 to 31, as said below
- directions: bfloat16 [8, 114688], P(None, 'cpg'), may hold values from -0.015625 to 0.015625
- step_sizes: float32 [8], replicated, may hold values from 0.05 to 1.5
- supports: int32 [8, 64], replicated, may hold values from 0 to 895, as said below
Outputs:
- new_directions: float32 [8, 114688], P(None, 'cpg')
- quotients: float32 [8], replicated
The draws below stay inside these ranges and needn't reach their ends.
Inputs may be any that keep to these rules, and one draw needn't show every extreme that they name: Every class from 0 to 31 labels at least one sample. `supports`: each row holds 64 different block indices.
All inputs are finite; a program needn't handle non-finite values.
Results may differ from the reference program's by a relative error of at most 0.0026.
Values sent between devices are 32-bit elements; how exact they have to be, the bound alone decides.
A program may use at most 64 MiB of HBM per device.

```python
import math
import jax
import jax.numpy as jnp
from jax import lax

CLASSES = 32
DIRS = 8
BLOCK = 128
KB = 64
SAMPLES = 512
P_SIZE = 114688


def draw_methylation(key, part):
    base_key = jax.random.fold_in(key, 37)
    block_groups = P_SIZE // BLOCK
    latent_factor_rank = 4
    group_rows = 64
    random_key_list = jax.random.split(base_key, 6)
    sample_factor = jax.random.normal(random_key_list[0], (SAMPLES, latent_factor_rank), jnp.float32)
    site_factor = jax.random.normal(random_key_list[1], (latent_factor_rank, P_SIZE), jnp.float32)
    signal_spikes = jax.random.bernoulli(random_key_list[2], 0.4, (latent_factor_rank, block_groups)).astype(jnp.float32)
    signal_level = jax.random.uniform(random_key_list[3], (latent_factor_rank, block_groups), jnp.float32, 0.5, 2.0)
    block_signal_level = signal_spikes * signal_level
    block_norm = jnp.sqrt(1.0 + jnp.sum(block_signal_level * block_signal_level, axis=0))
    site_weight = jnp.repeat(block_signal_level / block_norm[None, :], BLOCK, axis=1) * site_factor
    site_scale = jnp.repeat(1.0 / block_norm, BLOCK)

    def one_group(index):
        rows = lax.dynamic_slice_in_dim(sample_factor, index * group_rows, group_rows, 0)
        perturbation_key = jax.random.fold_in(random_key_list[5], index)
        noise = jax.random.normal(perturbation_key, (group_rows, P_SIZE), jnp.float32)
        values = noise * site_scale[None, :] + jnp.dot(rows, site_weight)
        return jnp.clip(values, -6.0, 6.0).astype(jnp.bfloat16)
    stacked = lax.map(one_group, jnp.arange(SAMPLES // group_rows, dtype=jnp.int32))
    return stacked.reshape(SAMPLES, P_SIZE)


def draw_labels(key, part):
    first, second = jax.random.split(jax.random.fold_in(key, 11))
    drawn = jax.random.randint(first, (SAMPLES,), 0, CLASSES, dtype=jnp.int32)
    places = jax.random.permutation(second, SAMPLES)[:CLASSES]
    return drawn.at[places].set(jnp.arange(CLASSES, dtype=jnp.int32))


def draw_supports(key, part):
    block_groups = P_SIZE // BLOCK
    base = jax.random.fold_in(key, 23)
    first_row = jnp.concatenate([jnp.array([0, block_groups - 1], dtype=jnp.int32), (1 + jax.random.permutation(jax.random.fold_in(base, 0), block_groups - 2)[:KB - 2]).astype(jnp.int32)])
    others = [jax.random.permutation(jax.random.fold_in(base, 1 + row), block_groups)[:KB].astype(jnp.int32) for row in range(DIRS - 1)]
    return jnp.stack([first_row] + others, axis=0)


def block_levels(key, shape, shards, least, high):
    loudness = 1.0
    for axis_at, parts in shards:
        steps = jax.random.uniform(jax.random.fold_in(jax.random.fold_in(key, 6), axis_at), (parts,), jnp.float32, least / len(shards), high / len(shards))
        loudness = loudness * jnp.repeat(jnp.exp(steps), shape[axis_at] // parts).reshape((-1,) + (1,) * (len(shape) - 1 - axis_at))
    return loudness


def normal_values(rng, shape, spread, limit, cuts=(), kind=jnp.bfloat16):
    values = spread * jax.random.normal(rng, shape, jnp.float32)
    if cuts:
        values = values * block_levels(rng, shape, cuts, -0.22, 0.18)
    return jnp.clip(values, -limit, limit).astype(kind)


def setup_inputs(seed: int = 0) -> dict:
    streams_of = jax.random.split(jax.random.key(seed), 6)
    return {
        "methylation": draw_methylation(jax.random.fold_in(streams_of[5], 71), 0),
        "labels": draw_labels(jax.random.fold_in(streams_of[5], 71), 0),
        "directions": normal_values(streams_of[2], (DIRS, P_SIZE), P_SIZE ** -0.5, 0.015625, ((1, 16),)),
        "step_sizes": jnp.clip(jnp.exp(jax.random.uniform(streams_of[3], (DIRS,), jnp.float32, math.log(0.05), math.log(1.5))), 0.05, 1.5),
        "supports": draw_supports(jax.random.fold_in(streams_of[5], 71), 0),
    }


STABILITY_FLOOR = 1e-06

def block_mask(supports, first_block, count):
    block_ids = first_block + jnp.arange(count, dtype=jnp.int32)
    hits = jnp.any(supports[:, :, None] == block_ids[None, None, :], axis=1)
    return jnp.repeat(hits.astype(jnp.float32), BLOCK, axis=1)

def reference(methylation, labels, directions, step_sizes, supports):
    highest = lax.Precision.HIGHEST
    onehot = (labels[:, None] == jnp.arange(CLASSES, dtype=jnp.int32)[None, :]).astype(jnp.float32)
    projected = lax.dot_general(methylation, directions, (((1,), (1,)), ((), ())), preferred_element_type=jnp.float32)
    class_proj = jnp.dot(onehot.T, projected, precision=highest)
    counts = lax.optimization_barrier(jnp.sum(onehot, axis=0))
    mean_proj = class_proj / counts[:, None]
    within = projected - jnp.dot(onehot, mean_proj, precision=highest)
    within_q = lax.optimization_barrier(jnp.sum(within * within, axis=0))
    grand = lax.optimization_barrier(jnp.sum(class_proj, axis=0)) / SAMPLES
    between_q = lax.optimization_barrier(jnp.sum((mean_proj - grand[None, :]) * class_proj, axis=0))
    quotients = between_q / within_q
    combined = (jnp.dot(onehot, mean_proj - grand[None, :], precision=highest) - quotients[None, :] * within).astype(jnp.bfloat16)
    gradient = lax.dot_general(combined, methylation, (((0,), (0,)), ((), ())), preferred_element_type=jnp.float32)
    updated = directions.astype(jnp.float32) + (step_sizes / within_q)[:, None] * gradient
    masked = updated * block_mask(supports, 0, P_SIZE // BLOCK)
    mean_sq = lax.optimization_barrier(jnp.sum(masked * masked, axis=1)) / (KB * BLOCK)
    return (masked * lax.rsqrt(mean_sq + STABILITY_FLOOR)[:, None], quotients)
```

```python
import functools

import jax
import jax.numpy as jnp
from jax import lax
from jax.experimental import pallas as pl
from jax.experimental.pallas import tpu as pltpu
from jax.sharding import PartitionSpec as P

CLASSES = 32
BLOCK = 128
STABILITY_FLOOR = 1e-06
MESH = pl.DeviceIdType.MESH
F32 = jnp.float32
BF16 = jnp.bfloat16
NT = (((1,), (1,)), ((), ()))
NN = (((1,), (0,)), ((), ()))


def divisor(n, most):
    return max(d for d in range(1, most + 1) if n % d == 0)


def split3(x):
    high = x.astype(BF16).astype(F32)
    rest = x - high
    mid = rest.astype(BF16).astype(F32)
    return [high, mid, (rest - mid).astype(BF16).astype(F32)]


def eye_of(rows, lanes):
    return lax.broadcasted_iota(jnp.int32, (rows, lanes), 0) == lax.broadcasted_iota(
        jnp.int32, (rows, lanes), 1
    )


def to_row(col, lanes):
    rows = col.shape[0]
    return jnp.sum(jnp.where(eye_of(rows, lanes), col, 0.0), axis=0, keepdims=True)


def to_col(row, rows):
    return jnp.sum(jnp.where(eye_of(rows, row.shape[1]), row, 0.0), axis=1, keepdims=True)


def kernel(
    S, C, A, nk, nch,
    m_hbm, d_hbm, lab_ref, step_ref, sup_ref,
    out_ref, quo_ref,
    mv, dv, part, abuf, bbuf, pall, proj, lab_all, gsend, grecv, fbuf, sbuf, mask,
    m_sem, d_sem, lab_send, lab_recv, a_send, a_recv, b_send, b_recv, c_send, c_recv,
    g_send, g_recv, f_send, f_recv, s_send, s_recv,
):
    B = C // A
    N = S * C
    G = S * A
    rows, cols = mv.shape
    dirs = dv.shape[0]
    R = dirs // A
    ck = cols // nk
    piece = cols // S
    ch = piece // nch
    s = lax.axis_index("samp")
    c = lax.axis_index("cpg")
    a = lax.rem(c, A)
    b = lax.div(c, A)
    me = s * C + c
    mine = s * A + a

    d_copy = pltpu.make_async_copy(d_hbm, dv, d_sem)
    d_copy.start()
    m_copies = []
    for k in range(nk):
        span = pl.ds(k * ck, ck)
        copy = pltpu.make_async_copy(m_hbm.at[:, span], mv.at[:, span], m_sem.at[k])
        copy.start()
        m_copies.append(copy)

    barrier = pltpu.get_barrier_semaphore()

    def greet(r, carry):
        t = lax.rem(me + r, N)
        pl.semaphore_signal(
            barrier, inc=1, device_id=(lax.div(t, C), lax.rem(t, C)), device_id_type=MESH
        )
        return carry

    lax.fori_loop(1, N, greet, 0)

    lab_all[s] = lab_ref[...]
    sup = sup_ref[...]
    first = c * (cols // BLOCK) + s * (piece // BLOCK)
    for k in range(nch):
        for j in range(ch // BLOCK):
            hit = jnp.max(
                jnp.where(sup == first + (k * (ch // BLOCK) + j), 1.0, 0.0), axis=1, keepdims=True
            )
            mask[k, :, j * BLOCK:(j + 1) * BLOCK] = jnp.broadcast_to(hit, (dirs, BLOCK))

    d_copy.wait()
    acc = jnp.zeros((dirs, rows), F32)
    for k in range(nk):
        m_copies[k].wait()
        acc = acc + lax.dot_general(
            dv[:, k * ck:(k + 1) * ck], mv[:, k * ck:(k + 1) * ck], NT, preferred_element_type=F32
        )
    for i in range(A):
        part[i] = acc[i * R:(i + 1) * R, :]

    pl.semaphore_wait(barrier, N - 1)

    def remote(src, dst, send, recv, to):
        return pltpu.make_async_remote_copy(
            src_ref=src, dst_ref=dst, send_sem=send, recv_sem=recv, device_id=to,
            device_id_type=MESH,
        )

    sent = []

    def start(copy):
        copy.start()
        sent.append(copy)

    for r in range(1, A):
        t = lax.rem(a + r, A)
        start(remote(part.at[t], abuf.at[a], a_send.at[r], a_recv.at[a], (s, b * A + t)))
    for r in range(1, S):
        t = lax.rem(s + r, S)
        start(remote(lab_ref, lab_all.at[s], lab_send.at[r], lab_recv.at[s], (t, c)))
    abuf[a] = part[a]
    for r in range(1, A):
        t = lax.rem(a + r, A)
        remote(part.at[t], abuf.at[t], a_send.at[r], a_recv.at[t], (s, c)).wait_recv()
    bbuf[b] = functools.reduce(jnp.add, [abuf[i] for i in range(A)])
    for r in range(1, B):
        t = lax.rem(b + r, B)
        start(remote(bbuf.at[b], bbuf.at[b], b_send.at[r], b_recv.at[b], (s, t * A + a)))
    for r in range(1, B):
        t = lax.rem(b + r, B)
        remote(bbuf.at[t], bbuf.at[t], b_send.at[r], b_recv.at[t], (s, c)).wait_recv()
    pall[mine] = functools.reduce(jnp.add, [bbuf[i] for i in range(B)])
    for r in range(1, G):
        t = lax.rem(mine + r, G)
        to = (lax.div(t, A), b * A + lax.rem(t, A))
        start(remote(pall.at[mine], pall.at[mine], c_send.at[r], c_recv.at[mine], to))
    for r in range(1, S):
        t = lax.rem(s + r, S)
        remote(lab_ref, lab_all.at[t], lab_send.at[r], lab_recv.at[t], (s, c)).wait_recv()
    classes = lax.broadcasted_iota(jnp.int32, (CLASSES, rows), 0)
    onehot = [(classes == lab_all[i]).astype(F32).astype(BF16) for i in range(S)]
    for r in range(1, G):
        t = lax.rem(mine + r, G)
        remote(pall.at[t], pall.at[t], c_send.at[r], c_recv.at[t], (s, c)).wait_recv()

    stats = jnp.zeros((4 * dirs, CLASSES), F32)
    for i in range(S):
        for j in range(A):
            proj[i, j * R:(j + 1) * R, :] = pall[i * A + j]
        left = jnp.concatenate(split3(proj[i]) + [jnp.ones((dirs, rows), F32)], axis=0)
        stats = stats + lax.dot_general(left.astype(BF16), onehot[i], NT, preferred_element_type=F32)
    class_proj = stats[:dirs] + stats[dirs:2 * dirs] + stats[2 * dirs:3 * dirs]
    mean_proj = class_proj / stats[3 * dirs:]
    grand = jnp.sum(class_proj, axis=1, keepdims=True) / (S * rows)
    between_q = jnp.sum((mean_proj - grand) * class_proj, axis=1, keepdims=True)
    left = jnp.concatenate(split3(mean_proj), axis=0).astype(BF16)

    def expand(hot):
        e = lax.dot_general(left, hot, NN, preferred_element_type=F32)
        return e[:dirs] + e[dirs:2 * dirs] + e[2 * dirs:]

    squares = jnp.zeros((dirs, rows), F32)
    for i in range(S):
        within = proj[i] - expand(onehot[i])
        squares = squares + within * within
    within_q = jnp.sum(squares, axis=1, keepdims=True)
    quotients = between_q / within_q
    own = expand((classes == lab_ref[...]).astype(F32).astype(BF16))
    combined = ((own - grand) - quotients * (proj[s] - own)).astype(BF16)
    scale = to_col(step_ref[...], dirs) / within_q
    quo_ref[...] = to_row(quotients, dirs)

    for r in list(range(1, S)) + [0]:
        t = lax.rem(s + r, S)
        for k in range(nch):
            span = pl.ds(pl.multiple_of(t * piece + k * ch, BLOCK), ch)
            g = jnp.dot(combined, mv[:, span], preferred_element_type=F32)
            if r == 0:
                grecv[s, k] = g
            else:
                gsend[r - 1, k] = g
                start(remote(
                    gsend.at[r - 1, k], grecv.at[s, k], g_send.at[r, k], g_recv.at[s, k], (t, c)
                ))
    total = jnp.zeros((dirs, ch), F32)
    for k in range(nch):
        for r in range(1, S):
            t = lax.rem(s + r, S)
            remote(
                gsend.at[r - 1, k], grecv.at[t, k], g_send.at[r, k], g_recv.at[t, k], (s, c)
            ).wait_recv()
        g = functools.reduce(jnp.add, [grecv[i, k] for i in range(S)])
        span = pl.ds(pl.multiple_of(s * piece + k * ch, BLOCK), ch)
        kept = (dv[:, span].astype(F32) + scale * g) * mask[k]
        fbuf[s, k] = kept
        total = total + kept * kept
    sbuf[me] = to_row(jnp.sum(total, axis=1, keepdims=True), BLOCK)

    def tell(r, carry):
        t = lax.rem(me + r, N)
        remote(
            sbuf.at[me], sbuf.at[me], s_send, s_recv, (lax.div(t, C), lax.rem(t, C))
        ).start()
        return carry

    lax.fori_loop(1, N, tell, 0)
    for r in range(1, S):
        t = lax.rem(s + r, S)
        start(remote(fbuf.at[s], fbuf.at[s], f_send.at[r], f_recv.at[s], (t, c)))
    others = sbuf.at[pl.ds(0, N - 1)]
    pltpu.make_async_copy(others, others, s_recv).wait()
    sums = to_col(jnp.sum(sbuf[...], axis=0), dirs)
    norm = lax.rsqrt(sums / (sup_ref.shape[1] * BLOCK) + STABILITY_FLOOR)
    for r in range(1, S):
        t = lax.rem(s + r, S)
        remote(fbuf.at[t], fbuf.at[t], f_send.at[r], f_recv.at[t], (s, c)).wait_recv()
    for i in range(S):
        for k in range(nch):
            at = i * piece + k * ch
            out_ref[:, at:at + ch] = fbuf[i, k] * norm
    for copy in sent:
        copy.wait_send()
    pltpu.make_async_copy(others, others, s_send).wait()


def per_device(S, C, methylation, labels, directions, step_sizes, supports):
    rows, cols = methylation.shape
    dirs = directions.shape[0]
    A = max(d for d in range(1, dirs + 1) if dirs % d == 0 and C % d == 0 and d * d <= C)
    B, N, G, R = C // A, S * C, S * A, dirs // A
    piece = cols // S
    nk = divisor(cols // BLOCK, 7)
    nch = divisor(piece // BLOCK, 4)
    ch = piece // nch
    dma = pltpu.SemaphoreType.DMA
    vmem = pl.BlockSpec(memory_space=pltpu.VMEM)
    hbm = pl.BlockSpec(memory_space=pltpu.HBM)
    out, quotients = pl.pallas_call(
        functools.partial(kernel, S, C, A, nk, nch),
        out_shape=(
            jax.ShapeDtypeStruct((dirs, cols), F32),
            jax.ShapeDtypeStruct((1, dirs), F32),
        ),
        in_specs=[hbm, hbm, vmem, vmem, vmem],
        out_specs=(vmem, vmem),
        scratch_shapes=[
            pltpu.VMEM((rows, cols), BF16),
            pltpu.VMEM((dirs, cols), BF16),
            pltpu.VMEM((A, R, rows), F32),
            pltpu.VMEM((A, R, rows), F32),
            pltpu.VMEM((B, R, rows), F32),
            pltpu.VMEM((G, R, rows), F32),
            pltpu.VMEM((S, dirs, rows), F32),
            pltpu.VMEM((S, 1, rows), jnp.int32),
            pltpu.VMEM((max(S - 1, 1), nch, dirs, ch), F32),
            pltpu.VMEM((S, nch, dirs, ch), F32),
            pltpu.VMEM((S, nch, dirs, ch), F32),
            pltpu.VMEM((N, 1, BLOCK), F32),
            pltpu.VMEM((nch, dirs, ch), F32),
            dma((nk,)), dma, dma((S,)), dma((S,)), dma((A,)), dma((A,)), dma((B,)), dma((B,)),
            dma((G,)), dma((G,)), dma((S, nch)), dma((S, nch)), dma((S,)), dma((S,)), dma, dma,
        ],
        compiler_params=pltpu.CompilerParams(
            collective_id=0, has_side_effects=True, vmem_limit_bytes=67_000_000
        ),
        name="flow_step",
    )(methylation, directions, labels.reshape(1, rows), step_sizes.reshape(1, dirs), supports)
    return out, quotients.reshape(dirs)


def solution(mesh):
    in_specs = (P("samp", "cpg"), P("samp"), P(None, "cpg"), P(), P())
    out_specs = (P(None, "cpg"), P())
    return jax.shard_map(
        functools.partial(per_device, mesh.shape["samp"], mesh.shape["cpg"]),
        mesh=mesh, in_specs=in_specs, out_specs=out_specs, check_vma=False,
    )
```

```python
import functools

import jax
import jax.numpy as jnp
from jax import lax
from jax.experimental import pallas as pl
from jax.experimental.pallas import tpu as pltpu
from jax.sharding import PartitionSpec as P

CLASSES = 32
BLOCK = 128
STABILITY_FLOOR = 1e-06
MESH = pl.DeviceIdType.MESH
F32 = jnp.float32
BF16 = jnp.bfloat16
NT = (((1,), (1,)), ((), ()))
NN = (((1,), (0,)), ((), ()))


def divisor(n, most):
    return max(d for d in range(1, most + 1) if n % d == 0)


def split3(x):
    high = x.astype(BF16).astype(F32)
    rest = x - high
    mid = rest.astype(BF16).astype(F32)
    return [high, mid, (rest - mid).astype(BF16).astype(F32)]


def eye_of(rows, lanes):
    return lax.broadcasted_iota(jnp.int32, (rows, lanes), 0) == lax.broadcasted_iota(
        jnp.int32, (rows, lanes), 1
    )


def to_row(col, lanes):
    rows = col.shape[0]
    return jnp.sum(jnp.where(eye_of(rows, lanes), col, 0.0), axis=0, keepdims=True)


def to_col(row, rows):
    return jnp.sum(jnp.where(eye_of(rows, row.shape[1]), row, 0.0), axis=1, keepdims=True)


def kernel(
    S, C, A, nk, nch,
    m_hbm, d_hbm, lab_ref, step_ref, sup_ref,
    kept_hbm, norm_ref, quo_ref,
    mv, dv, part, abuf, bbuf, pall, proj, lab_all, gsend, grecv, fbuf, sbuf, mask,
    m_sem, d_sem, lab_send, lab_recv, a_send, a_recv, b_send, b_recv, c_send, c_recv,
    g_send, g_recv, f_send, f_recv, s_send, s_recv, o_sem,
):
    B = C // A
    N = S * C
    G = S * A
    rows, cols = mv.shape
    dirs = dv.shape[0]
    R = dirs // A
    ck = cols // nk
    piece = cols // S
    ch = piece // nch
    s = lax.axis_index("samp")
    c = lax.axis_index("cpg")
    a = lax.rem(c, A)
    b = lax.div(c, A)
    me = s * C + c
    mine = s * A + a

    barrier = pltpu.get_barrier_semaphore()
    partners = [(s, lax.rem(b + r, B) * A + a) for r in range(1, B)]
    partners += [(lax.rem(s + r, S), c) for r in range(1, S)]
    partners += [(s, b * A + lax.rem(a + r, A)) for r in range(1, A)]
    for partner in partners:
        pl.semaphore_signal(barrier, inc=1, device_id=partner, device_id_type=MESH)

    d_copy = pltpu.make_async_copy(d_hbm, dv, d_sem)
    d_copy.start()
    m_copies = []
    for k in range(nk):
        span = pl.ds(k * ck, ck)
        copy = pltpu.make_async_copy(m_hbm.at[:, span], mv.at[:, span], m_sem.at[k])
        copy.start()
        m_copies.append(copy)

    lab_all[s] = lab_ref[...]
    sup = sup_ref[...]
    first = c * (cols // BLOCK) + s * (piece // BLOCK)
    for k in range(nch):
        for j in range(ch // BLOCK):
            hit = jnp.max(
                jnp.where(sup == first + (k * (ch // BLOCK) + j), 1.0, 0.0), axis=1, keepdims=True
            )
            mask[k, :, j * BLOCK:(j + 1) * BLOCK] = jnp.broadcast_to(hit, (dirs, BLOCK))

    d_copy.wait()
    acc = jnp.zeros((dirs, rows), F32)
    for k in range(nk):
        m_copies[k].wait()
        acc = acc + lax.dot_general(
            dv[:, k * ck:(k + 1) * ck], mv[:, k * ck:(k + 1) * ck], NT, preferred_element_type=F32
        )
    for i in range(A):
        part[i] = acc[i * R:(i + 1) * R, :]

    pl.semaphore_wait(barrier, len(partners))

    def remote(src, dst, send, recv, to):
        return pltpu.make_async_remote_copy(
            src_ref=src, dst_ref=dst, send_sem=send, recv_sem=recv, device_id=to,
            device_id_type=MESH,
        )

    sent = []

    def start(copy):
        copy.start()
        sent.append(copy)

    for r in range(1, A):
        t = lax.rem(a + r, A)
        start(remote(part.at[t], abuf.at[a], a_send.at[r], a_recv.at[a], (s, b * A + t)))
    for r in range(1, S):
        t = lax.rem(s + r, S)
        start(remote(lab_ref, lab_all.at[s], lab_send.at[r], lab_recv.at[s], (t, c)))
    abuf[a] = part[a]
    for r in range(1, A):
        t = lax.rem(a + r, A)
        remote(part.at[t], abuf.at[t], a_send.at[r], a_recv.at[t], (s, c)).wait_recv()
    bbuf[b] = functools.reduce(jnp.add, [abuf[i] for i in range(A)])
    for r in range(1, B):
        t = lax.rem(b + r, B)
        start(remote(bbuf.at[b], bbuf.at[b], b_send.at[r], b_recv.at[b], (s, t * A + a)))
    for r in range(1, B):
        t = lax.rem(b + r, B)
        remote(bbuf.at[t], bbuf.at[t], b_send.at[r], b_recv.at[t], (s, c)).wait_recv()
    pall[mine] = functools.reduce(jnp.add, [bbuf[i] for i in range(B)])
    for r in range(1, G):
        t = lax.rem(mine + r, G)
        to = (lax.div(t, A), b * A + lax.rem(t, A))
        start(remote(pall.at[mine], pall.at[mine], c_send.at[r], c_recv.at[mine], to))
    for r in range(1, S):
        t = lax.rem(s + r, S)
        remote(lab_ref, lab_all.at[t], lab_send.at[r], lab_recv.at[t], (s, c)).wait_recv()
    classes = lax.broadcasted_iota(jnp.int32, (CLASSES, rows), 0)
    onehot = [(classes == lab_all[i]).astype(F32).astype(BF16) for i in range(S)]
    for r in range(1, G):
        t = lax.rem(mine + r, G)
        remote(pall.at[t], pall.at[t], c_send.at[r], c_recv.at[t], (s, c)).wait_recv()

    stats = jnp.zeros((4 * dirs, CLASSES), F32)
    for i in range(S):
        for j in range(A):
            proj[i, j * R:(j + 1) * R, :] = pall[i * A + j]
        left = jnp.concatenate(split3(proj[i]) + [jnp.ones((dirs, rows), F32)], axis=0)
        stats = stats + lax.dot_general(left.astype(BF16), onehot[i], NT, preferred_element_type=F32)
    class_proj = stats[:dirs] + stats[dirs:2 * dirs] + stats[2 * dirs:3 * dirs]
    mean_proj = class_proj / stats[3 * dirs:]
    grand = jnp.sum(class_proj, axis=1, keepdims=True) / (S * rows)
    between_q = jnp.sum((mean_proj - grand) * class_proj, axis=1, keepdims=True)
    left = jnp.concatenate(split3(mean_proj), axis=0).astype(BF16)

    def expand(hot):
        e = lax.dot_general(left, hot, NN, preferred_element_type=F32)
        return e[:dirs] + e[dirs:2 * dirs] + e[2 * dirs:]

    squares = jnp.zeros((dirs, rows), F32)
    for i in range(S):
        within = proj[i] - expand(onehot[i])
        squares = squares + within * within
    within_q = jnp.sum(squares, axis=1, keepdims=True)
    quotients = between_q / within_q
    own = expand((classes == lab_ref[...]).astype(F32).astype(BF16))
    combined = ((own - grand) - quotients * (proj[s] - own)).astype(BF16)
    scale = to_col(step_ref[...], dirs) / within_q
    quo_ref[...] = to_row(quotients, dirs)

    for r in list(range(1, S)) + [0]:
        t = lax.rem(s + r, S)
        for k in range(nch):
            span = pl.ds(pl.multiple_of(t * piece + k * ch, BLOCK), ch)
            g = jnp.dot(combined, mv[:, span], preferred_element_type=F32)
            if r == 0:
                grecv[s, k] = g
            else:
                gsend[r - 1, k] = g
                start(remote(
                    gsend.at[r - 1, k], grecv.at[s, k], g_send.at[r, k], g_recv.at[s, k], (t, c)
                ))
    total = jnp.zeros((dirs, ch), F32)
    for k in range(nch):
        for r in range(1, S):
            t = lax.rem(s + r, S)
            remote(
                gsend.at[r - 1, k], grecv.at[t, k], g_send.at[r, k], g_recv.at[t, k], (s, c)
            ).wait_recv()
        g = functools.reduce(jnp.add, [grecv[i, k] for i in range(S)])
        span = pl.ds(pl.multiple_of(s * piece + k * ch, BLOCK), ch)
        kept = (dv[:, span].astype(F32) + scale * g) * mask[k]
        fbuf[s, k] = kept
        total = total + kept * kept
    sbuf[me] = to_row(jnp.sum(total, axis=1, keepdims=True), BLOCK)

    def tell(r, carry):
        t = lax.rem(me + r, N)
        remote(
            sbuf.at[me], sbuf.at[me], s_send, s_recv, (lax.div(t, C), lax.rem(t, C))
        ).start()
        return carry

    if N <= 64:
        for r in range(1, N):
            tell(r, 0)
    else:
        lax.fori_loop(1, N, tell, 0)
    for r in range(1, S):
        t = lax.rem(s + r, S)
        start(remote(fbuf.at[s], fbuf.at[s], f_send.at[r], f_recv.at[s], (t, c)))
    out_copies = [pltpu.make_async_copy(fbuf.at[s], kept_hbm.at[s], o_sem.at[0])]
    out_copies[0].start()
    others = sbuf.at[pl.ds(0, N - 1)]
    for r in range(1, S):
        t = lax.rem(s + r, S)
        remote(fbuf.at[t], fbuf.at[t], f_send.at[r], f_recv.at[t], (s, c)).wait_recv()
        copy = pltpu.make_async_copy(fbuf.at[t], kept_hbm.at[t], o_sem.at[r])
        copy.start()
        out_copies.append(copy)
    pltpu.make_async_copy(others, others, s_recv).wait()
    sums = to_col(jnp.sum(sbuf[...], axis=0), dirs)
    norm = lax.rsqrt(sums / (sup_ref.shape[1] * BLOCK) + STABILITY_FLOOR)
    norm_ref[...] = jnp.broadcast_to(norm, (dirs, BLOCK))
    for copy in sent:
        copy.wait_send()
    pltpu.make_async_copy(others, others, s_send).wait()
    for copy in out_copies:
        copy.wait()


def finish(S, nch, ch, kept_ref, norm_ref, quo_in, out_ref, quo_ref):
    norm = norm_ref[:, :1]
    for i in range(S):
        for k in range(nch):
            at = (i * nch + k) * ch
            out_ref[:, at:at + ch] = kept_ref[i, k] * norm
    quo_ref[...] = quo_in[...]


def per_device(S, C, methylation, labels, directions, step_sizes, supports):
    rows, cols = methylation.shape
    dirs = directions.shape[0]
    A = max(d for d in range(1, dirs + 1) if dirs % d == 0 and C % d == 0 and d * d <= C)
    B, N, G, R = C // A, S * C, S * A, dirs // A
    piece = cols // S
    nk = divisor(cols // BLOCK, 7)
    nch = divisor(piece // BLOCK, 4)
    ch = piece // nch
    dma = pltpu.SemaphoreType.DMA
    vmem = pl.BlockSpec(memory_space=pltpu.VMEM)
    hbm = pl.BlockSpec(memory_space=pltpu.HBM)
    kept, norm, quotients = pl.pallas_call(
        functools.partial(kernel, S, C, A, nk, nch),
        out_shape=(
            jax.ShapeDtypeStruct((S, nch, dirs, ch), F32),
            jax.ShapeDtypeStruct((dirs, BLOCK), F32),
            jax.ShapeDtypeStruct((1, dirs), F32),
        ),
        in_specs=[hbm, hbm, vmem, vmem, vmem],
        out_specs=(hbm, vmem, vmem),
        scratch_shapes=[
            pltpu.VMEM((rows, cols), BF16),
            pltpu.VMEM((dirs, cols), BF16),
            pltpu.VMEM((A, R, rows), F32),
            pltpu.VMEM((A, R, rows), F32),
            pltpu.VMEM((B, R, rows), F32),
            pltpu.VMEM((G, R, rows), F32),
            pltpu.VMEM((S, dirs, rows), F32),
            pltpu.VMEM((S, 1, rows), jnp.int32),
            pltpu.VMEM((max(S - 1, 1), nch, dirs, ch), F32),
            pltpu.VMEM((S, nch, dirs, ch), F32),
            pltpu.VMEM((S, nch, dirs, ch), F32),
            pltpu.VMEM((N, 1, BLOCK), F32),
            pltpu.VMEM((nch, dirs, ch), F32),
            dma((nk,)), dma, dma((S,)), dma((S,)), dma((A,)), dma((A,)), dma((B,)), dma((B,)),
            dma((G,)), dma((G,)), dma((S, nch)), dma((S, nch)), dma((S,)), dma((S,)), dma, dma,
            dma((S,)),
        ],
        compiler_params=pltpu.CompilerParams(
            collective_id=0, has_side_effects=True, vmem_limit_bytes=67_000_000
        ),
        name="flow_step",
    )(methylation, directions, labels.reshape(1, rows), step_sizes.reshape(1, dirs), supports)
    out, quotients = pl.pallas_call(
        functools.partial(finish, S, nch, ch),
        out_shape=(
            jax.ShapeDtypeStruct((dirs, cols), F32),
            jax.ShapeDtypeStruct((1, dirs), F32),
        ),
        in_specs=[vmem, vmem, vmem],
        out_specs=(vmem, vmem),
        compiler_params=pltpu.CompilerParams(vmem_limit_bytes=67_000_000),
        name="finish",
    )(kept, norm, quotients)
    return out, quotients.reshape(dirs)


def solution(mesh):
    in_specs = (P("samp", "cpg"), P("samp"), P(None, "cpg"), P(), P())
    out_specs = (P(None, "cpg"), P())
    return jax.shard_map(
        functools.partial(per_device, mesh.shape["samp"], mesh.shape["cpg"]),
        mesh=mesh, in_specs=in_specs, out_specs=out_specs, check_vma=False,
    )
```

```python
import functools

import jax
import jax.numpy as jnp
from jax import lax
from jax.experimental import pallas as pl
from jax.experimental.pallas import tpu as pltpu
from jax.sharding import PartitionSpec as P

CLASSES = 32
BLOCK = 128
STABILITY_FLOOR = 1e-06
MESH = pl.DeviceIdType.MESH
F32 = jnp.float32
BF16 = jnp.bfloat16
NT = (((1,), (1,)), ((), ()))
NN = (((1,), (0,)), ((), ()))


def divisor(n, most):
    return max(d for d in range(1, most + 1) if n % d == 0)


def split3(x):
    high = x.astype(BF16).astype(F32)
    rest = x - high
    mid = rest.astype(BF16).astype(F32)
    return [high, mid, (rest - mid).astype(BF16).astype(F32)]


def eye_of(rows, lanes):
    return lax.broadcasted_iota(jnp.int32, (rows, lanes), 0) == lax.broadcasted_iota(
        jnp.int32, (rows, lanes), 1
    )


def to_row(col, lanes):
    rows = col.shape[0]
    return jnp.sum(jnp.where(eye_of(rows, lanes), col, 0.0), axis=0, keepdims=True)


def to_col(row, rows):
    return jnp.sum(jnp.where(eye_of(rows, row.shape[1]), row, 0.0), axis=1, keepdims=True)


def kernel(
    S, C, A, nk, nch,
    m_hbm, d_hbm, lab_ref, step_ref, sup_ref,
    kept_hbm, norm_ref, quo_ref,
    mv, dv, part, abuf, bbuf, pall, proj, lab_all, gsend, grecv, fbuf, sbuf, mask,
    m_sem, d_sem, lab_send, lab_recv, a_send, a_recv, b_send, b_recv, c_send, c_recv,
    g_send, g_recv, f_send, f_recv, s_send, s_recv, o_sem,
):
    B = C // A
    N = S * C
    G = S * A
    rows, cols = mv.shape
    dirs = dv.shape[0]
    R = dirs // A
    ck = cols // nk
    piece = cols // S
    ch = piece // nch
    s = lax.axis_index("samp")
    c = lax.axis_index("cpg")
    a = lax.rem(c, A)
    b = lax.div(c, A)
    me = s * C + c
    mine = s * A + a

    barrier = pltpu.get_barrier_semaphore()
    partners = [(s, lax.rem(b + r, B) * A + a) for r in range(1, B)]
    partners += [(lax.rem(s + r, S), c) for r in range(1, S)]
    partners += [(s, b * A + lax.rem(a + r, A)) for r in range(1, A)]
    for partner in partners:
        pl.semaphore_signal(barrier, inc=1, device_id=partner, device_id_type=MESH)

    d_copy = pltpu.make_async_copy(d_hbm, dv, d_sem)
    d_copy.start()
    m_copies = []
    for k in range(nk):
        span = pl.ds(k * ck, ck)
        copy = pltpu.make_async_copy(m_hbm.at[:, span], mv.at[:, span], m_sem.at[k])
        copy.start()
        m_copies.append(copy)

    lab_all[s] = lab_ref[...]
    sup = sup_ref[...]
    first = c * (cols // BLOCK) + s * (piece // BLOCK)
    for k in range(nch):
        for j in range(ch // BLOCK):
            hit = jnp.max(
                jnp.where(sup == first + (k * (ch // BLOCK) + j), 1.0, 0.0), axis=1, keepdims=True
            )
            mask[k, :, j * BLOCK:(j + 1) * BLOCK] = jnp.broadcast_to(hit, (dirs, BLOCK))

    d_copy.wait()
    acc = jnp.zeros((dirs, rows), F32)
    for k in range(nk):
        m_copies[k].wait()
        acc = acc + lax.dot_general(
            dv[:, k * ck:(k + 1) * ck], mv[:, k * ck:(k + 1) * ck], NT, preferred_element_type=F32
        )
    for i in range(A):
        part[i] = acc[i * R:(i + 1) * R, :]

    pl.semaphore_wait(barrier, len(partners))

    def remote(src, dst, send, recv, to):
        return pltpu.make_async_remote_copy(
            src_ref=src, dst_ref=dst, send_sem=send, recv_sem=recv, device_id=to,
            device_id_type=MESH,
        )

    sent = []

    def start(copy):
        copy.start()
        sent.append(copy)

    for r in range(1, A):
        t = lax.rem(a + r, A)
        start(remote(part.at[t], abuf.at[a], a_send.at[r], a_recv.at[a], (s, b * A + t)))
    for r in range(1, S):
        t = lax.rem(s + r, S)
        start(remote(lab_ref, lab_all.at[s], lab_send.at[r], lab_recv.at[s], (t, c)))
    abuf[a] = part[a]
    for r in range(1, A):
        t = lax.rem(a + r, A)
        remote(part.at[t], abuf.at[t], a_send.at[r], a_recv.at[t], (s, c)).wait_recv()
    bbuf[b] = functools.reduce(jnp.add, [abuf[i] for i in range(A)])
    for r in range(1, B):
        t = lax.rem(b + r, B)
        start(remote(bbuf.at[b], bbuf.at[b], b_send.at[r], b_recv.at[b], (s, t * A + a)))
    for r in range(1, B):
        t = lax.rem(b + r, B)
        remote(bbuf.at[t], bbuf.at[t], b_send.at[r], b_recv.at[t], (s, c)).wait_recv()
    pall[mine] = functools.reduce(jnp.add, [bbuf[i] for i in range(B)])
    for r in range(1, G):
        t = lax.rem(mine + r, G)
        to = (lax.div(t, A), b * A + lax.rem(t, A))
        start(remote(pall.at[mine], pall.at[mine], c_send.at[r], c_recv.at[mine], to))
    for r in range(1, S):
        t = lax.rem(s + r, S)
        remote(lab_ref, lab_all.at[t], lab_send.at[r], lab_recv.at[t], (s, c)).wait_recv()
    classes = lax.broadcasted_iota(jnp.int32, (CLASSES, rows), 0)
    onehot = [(classes == lab_all[i]).astype(F32).astype(BF16) for i in range(S)]
    for r in range(1, G):
        t = lax.rem(mine + r, G)
        remote(pall.at[t], pall.at[t], c_send.at[r], c_recv.at[t], (s, c)).wait_recv()

    stats = jnp.zeros((4 * dirs, CLASSES), F32)
    for i in range(S):
        for j in range(A):
            proj[i, j * R:(j + 1) * R, :] = pall[i * A + j]
        left = jnp.concatenate(split3(proj[i]) + [jnp.ones((dirs, rows), F32)], axis=0)
        stats = stats + lax.dot_general(left.astype(BF16), onehot[i], NT, preferred_element_type=F32)
    class_proj = stats[:dirs] + stats[dirs:2 * dirs] + stats[2 * dirs:3 * dirs]
    mean_proj = class_proj / stats[3 * dirs:]
    grand = jnp.sum(class_proj, axis=1, keepdims=True) / (S * rows)
    between_q = jnp.sum((mean_proj - grand) * class_proj, axis=1, keepdims=True)
    left = jnp.concatenate(split3(mean_proj), axis=0).astype(BF16)

    def expand(hot):
        e = lax.dot_general(left, hot, NN, preferred_element_type=F32)
        return e[:dirs] + e[dirs:2 * dirs] + e[2 * dirs:]

    squares = jnp.zeros((dirs, rows), F32)
    for i in range(S):
        within = proj[i] - expand(onehot[i])
        squares = squares + within * within
    within_q = jnp.sum(squares, axis=1, keepdims=True)
    quotients = between_q / within_q
    own = expand((classes == lab_ref[...]).astype(F32).astype(BF16))
    combined = ((own - grand) - quotients * (proj[s] - own)).astype(BF16)
    scale = to_col(step_ref[...], dirs) / within_q
    quo_ref[...] = to_row(quotients, dirs)

    for r in list(range(1, S)) + [0]:
        t = lax.rem(s + r, S)
        for k in range(nch):
            span = pl.ds(pl.multiple_of(t * piece + k * ch, BLOCK), ch)
            g = jnp.dot(combined, mv[:, span], preferred_element_type=F32)
            if r == 0:
                grecv[s, k] = g
            else:
                gsend[r - 1, k] = g
                start(remote(
                    gsend.at[r - 1, k], grecv.at[s, k], g_send.at[r, k], g_recv.at[s, k], (t, c)
                ))
    total = jnp.zeros((dirs, ch), F32)
    for k in range(nch):
        for r in range(1, S):
            t = lax.rem(s + r, S)
            remote(
                gsend.at[r - 1, k], grecv.at[t, k], g_send.at[r, k], g_recv.at[t, k], (s, c)
            ).wait_recv()
        g = functools.reduce(jnp.add, [grecv[i, k] for i in range(S)])
        span = pl.ds(pl.multiple_of(s * piece + k * ch, BLOCK), ch)
        kept = (dv[:, span].astype(F32) + scale * g) * mask[k]
        fbuf[s, k] = kept
        total = total + kept * kept
    sbuf[me] = to_row(jnp.sum(total, axis=1, keepdims=True), BLOCK)

    def tell(r, carry):
        t = lax.rem(me + r, N)
        remote(
            sbuf.at[me], sbuf.at[me], s_send, s_recv, (lax.div(t, C), lax.rem(t, C))
        ).start()
        return carry

    if N <= 64:
        for r in range(1, N):
            tell(r, 0)
    else:
        lax.fori_loop(1, N, tell, 0)
    for r in range(1, S):
        t = lax.rem(s + r, S)
        start(remote(fbuf.at[s], fbuf.at[s], f_send.at[r], f_recv.at[s], (t, c)))
    out_copies = [pltpu.make_async_copy(fbuf.at[s], kept_hbm.at[s], o_sem.at[0])]
    out_copies[0].start()
    others = sbuf.at[pl.ds(0, N - 1)]
    for r in range(1, S):
        t = lax.rem(s + r, S)
        remote(fbuf.at[t], fbuf.at[t], f_send.at[r], f_recv.at[t], (s, c)).wait_recv()
        copy = pltpu.make_async_copy(fbuf.at[t], kept_hbm.at[t], o_sem.at[r])
        copy.start()
        out_copies.append(copy)
    pltpu.make_async_copy(others, others, s_recv).wait()
    sums = to_col(jnp.sum(sbuf[...], axis=0), dirs)
    norm = lax.rsqrt(sums / (sup_ref.shape[1] * BLOCK) + STABILITY_FLOOR)
    norm_ref[...] = jnp.broadcast_to(norm, (dirs, BLOCK))
    for copy in sent:
        copy.wait_send()
    pltpu.make_async_copy(others, others, s_send).wait()
    for copy in out_copies:
        copy.wait()


def finish(S, nch, ch, kept_ref, norm_ref, quo_in, out_ref, quo_ref):
    norm = norm_ref[:, :1]
    for i in range(S):
        for k in range(nch):
            at = (i * nch + k) * ch
            out_ref[:, at:at + ch] = kept_ref[i, k] * norm
    quo_ref[...] = quo_in[...]


def per_device(S, C, methylation, labels, directions, step_sizes, supports):
    rows, cols = methylation.shape
    dirs = directions.shape[0]
    A = max(d for d in range(1, dirs + 1) if dirs % d == 0 and C % d == 0 and d * d * d <= C)
    B, N, G, R = C // A, S * C, S * A, dirs // A
    piece = cols // S
    nk = divisor(cols // BLOCK, 7)
    nch = divisor(piece // BLOCK, 4)
    ch = piece // nch
    dma = pltpu.SemaphoreType.DMA
    vmem = pl.BlockSpec(memory_space=pltpu.VMEM)
    hbm = pl.BlockSpec(memory_space=pltpu.HBM)
    kept, norm, quotients = pl.pallas_call(
        functools.partial(kernel, S, C, A, nk, nch),
        out_shape=(
            jax.ShapeDtypeStruct((S, nch, dirs, ch), F32),
            jax.ShapeDtypeStruct((dirs, BLOCK), F32),
            jax.ShapeDtypeStruct((1, dirs), F32),
        ),
        in_specs=[hbm, hbm, vmem, vmem, vmem],
        out_specs=(hbm, vmem, vmem),
        scratch_shapes=[
            pltpu.VMEM((rows, cols), BF16),
            pltpu.VMEM((dirs, cols), BF16),
            pltpu.VMEM((A, R, rows), F32),
            pltpu.VMEM((A, R, rows), F32),
            pltpu.VMEM((B, R, rows), F32),
            pltpu.VMEM((G, R, rows), F32),
            pltpu.VMEM((S, dirs, rows), F32),
            pltpu.VMEM((S, 1, rows), jnp.int32),
            pltpu.VMEM((max(S - 1, 1), nch, dirs, ch), F32),
            pltpu.VMEM((S, nch, dirs, ch), F32),
            pltpu.VMEM((S, nch, dirs, ch), F32),
            pltpu.VMEM((N, 1, BLOCK), F32),
            pltpu.VMEM((nch, dirs, ch), F32),
            dma((nk,)), dma, dma((S,)), dma((S,)), dma((A,)), dma((A,)), dma((B,)), dma((B,)),
            dma((G,)), dma((G,)), dma((S, nch)), dma((S, nch)), dma((S,)), dma((S,)), dma, dma,
            dma((S,)),
        ],
        compiler_params=pltpu.CompilerParams(
            collective_id=0, has_side_effects=True, vmem_limit_bytes=67_000_000
        ),
        name="flow_step",
    )(methylation, directions, labels.reshape(1, rows), step_sizes.reshape(1, dirs), supports)
    out, quotients = pl.pallas_call(
        functools.partial(finish, S, nch, ch),
        out_shape=(
            jax.ShapeDtypeStruct((dirs, cols), F32),
            jax.ShapeDtypeStruct((1, dirs), F32),
        ),
        in_specs=[vmem, vmem, vmem],
        out_specs=(vmem, vmem),
        compiler_params=pltpu.CompilerParams(vmem_limit_bytes=67_000_000),
        name="finish",
    )(kept, norm, quotients)
    return out, quotients.reshape(dirs)


def solution(mesh):
    in_specs = (P("samp", "cpg"), P("samp"), P(None, "cpg"), P(), P())
    out_specs = (P(None, "cpg"), P())
    return jax.shard_map(
        functools.partial(per_device, mesh.shape["samp"], mesh.shape["cpg"]),
        mesh=mesh, in_specs=in_specs, out_specs=out_specs, check_vma=False,
    )
```

```python
import functools

import jax
import jax.numpy as jnp
from jax import lax
from jax.experimental import pallas as pl
from jax.experimental.pallas import tpu as pltpu
from jax.sharding import PartitionSpec as P

CLASSES = 32
BLOCK = 128
STABILITY_FLOOR = 1e-06
MESH = pl.DeviceIdType.MESH
F32 = jnp.float32
BF16 = jnp.bfloat16
NT = (((1,), (1,)), ((), ()))
NN = (((1,), (0,)), ((), ()))


def divisor(n, most):
    return max(d for d in range(1, most + 1) if n % d == 0)


def split3(x):
    high = x.astype(BF16).astype(F32)
    rest = x - high
    mid = rest.astype(BF16).astype(F32)
    return [high, mid, (rest - mid).astype(BF16).astype(F32)]


def eye_of(rows, lanes):
    return lax.broadcasted_iota(jnp.int32, (rows, lanes), 0) == lax.broadcasted_iota(
        jnp.int32, (rows, lanes), 1
    )


def to_row(col, lanes):
    rows = col.shape[0]
    return jnp.sum(jnp.where(eye_of(rows, lanes), col, 0.0), axis=0, keepdims=True)


def to_col(row, rows):
    return jnp.sum(jnp.where(eye_of(rows, row.shape[1]), row, 0.0), axis=1, keepdims=True)


def kernel(
    S, C, A, nk, nch,
    m_hbm, d_hbm, lab_ref, step_ref, sup_ref,
    kept_hbm, norm_ref, quo_ref,
    mv, dv, part, abuf, bbuf, pall, proj, lab_all, gsend, grecv, fbuf, sbuf, mask,
    m_sem, d_sem, lab_send, lab_recv, a_send, a_recv, b_send, b_recv, c_send, c_recv,
    g_send, g_recv, f_send, f_recv, s_send, s_recv, o_sem,
):
    B = C // A
    N = S * C
    G = S * A
    rows, cols = mv.shape
    dirs = dv.shape[0]
    R = dirs // A
    ck = cols // nk
    piece = cols // S
    ch = piece // nch
    s = lax.axis_index("samp")
    c = lax.axis_index("cpg")
    a = lax.rem(c, A)
    b = lax.div(c, A)
    me = s * C + c
    mine = s * A + a

    barrier = pltpu.get_barrier_semaphore()
    partners = [(s, lax.rem(b + r, B) * A + a) for r in range(1, B)]
    partners += [(lax.rem(s + r, S), c) for r in range(1, S)]
    partners += [(s, b * A + lax.rem(a + r, A)) for r in range(1, A)]
    for partner in partners:
        pl.semaphore_signal(barrier, inc=1, device_id=partner, device_id_type=MESH)

    d_copy = pltpu.make_async_copy(d_hbm, dv, d_sem)
    d_copy.start()
    m_copies = []
    for k in range(nk):
        span = pl.ds(k * ck, ck)
        copy = pltpu.make_async_copy(m_hbm.at[:, span], mv.at[:, span], m_sem.at[k])
        copy.start()
        m_copies.append(copy)

    lab_all[s] = lab_ref[...]
    sup = sup_ref[...]
    first = c * (cols // BLOCK) + s * (piece // BLOCK)
    for k in range(nch):
        for j in range(ch // BLOCK):
            hit = jnp.max(
                jnp.where(sup == first + (k * (ch // BLOCK) + j), 1.0, 0.0), axis=1, keepdims=True
            )
            mask[k, :, j * BLOCK:(j + 1) * BLOCK] = jnp.broadcast_to(hit, (dirs, BLOCK))

    d_copy.wait()
    acc = jnp.zeros((dirs, rows), F32)
    for k in range(nk):
        m_copies[k].wait()
        acc = acc + lax.dot_general(
            dv[:, k * ck:(k + 1) * ck], mv[:, k * ck:(k + 1) * ck], NT, preferred_element_type=F32
        )
    for i in range(A):
        part[i] = acc[i * R:(i + 1) * R, :]

    pl.semaphore_wait(barrier, len(partners))

    def remote(src, dst, send, recv, to):
        return pltpu.make_async_remote_copy(
            src_ref=src, dst_ref=dst, send_sem=send, recv_sem=recv, device_id=to,
            device_id_type=MESH,
        )

    sent = []

    def start(copy):
        copy.start()
        sent.append(copy)

    for r in range(1, A):
        t = lax.rem(a + r, A)
        start(remote(part.at[t], abuf.at[a], a_send.at[r], a_recv.at[a], (s, b * A + t)))
    for r in range(1, S):
        t = lax.rem(s + r, S)
        start(remote(lab_ref, lab_all.at[s], lab_send.at[r], lab_recv.at[s], (t, c)))
    abuf[a] = part[a]
    for r in range(1, A):
        t = lax.rem(a + r, A)
        remote(part.at[t], abuf.at[t], a_send.at[r], a_recv.at[t], (s, c)).wait_recv()
    bbuf[b] = functools.reduce(jnp.add, [abuf[i] for i in range(A)])
    for r in range(1, B):
        t = lax.rem(b + r, B)
        start(remote(bbuf.at[b], bbuf.at[b], b_send.at[r], b_recv.at[b], (s, t * A + a)))
    for r in range(1, B):
        t = lax.rem(b + r, B)
        remote(bbuf.at[t], bbuf.at[t], b_send.at[r], b_recv.at[t], (s, c)).wait_recv()
    pall[mine] = functools.reduce(jnp.add, [bbuf[i] for i in range(B)])
    for r in range(1, G):
        t = lax.rem(mine + r, G)
        to = (lax.div(t, A), b * A + lax.rem(t, A))
        start(remote(pall.at[mine], pall.at[mine], c_send.at[r], c_recv.at[mine], to))
    for r in range(1, S):
        t = lax.rem(s + r, S)
        remote(lab_ref, lab_all.at[t], lab_send.at[r], lab_recv.at[t], (s, c)).wait_recv()
    classes = lax.broadcasted_iota(jnp.int32, (CLASSES, rows), 0)
    onehot = [(classes == lab_all[i]).astype(F32).astype(BF16) for i in range(S)]
    for r in range(1, G):
        t = lax.rem(mine + r, G)
        remote(pall.at[t], pall.at[t], c_send.at[r], c_recv.at[t], (s, c)).wait_recv()

    stats = jnp.zeros((4 * dirs, CLASSES), F32)
    for i in range(S):
        for j in range(A):
            proj[i, j * R:(j + 1) * R, :] = pall[i * A + j]
        left = jnp.concatenate(split3(proj[i]) + [jnp.ones((dirs, rows), F32)], axis=0)
        stats = stats + lax.dot_general(left.astype(BF16), onehot[i], NT, preferred_element_type=F32)
    class_proj = stats[:dirs] + stats[dirs:2 * dirs] + stats[2 * dirs:3 * dirs]
    mean_proj = class_proj / stats[3 * dirs:]
    grand = jnp.sum(class_proj, axis=1, keepdims=True) / (S * rows)
    between_q = jnp.sum((mean_proj - grand) * class_proj, axis=1, keepdims=True)
    left = jnp.concatenate(split3(mean_proj), axis=0).astype(BF16)

    def expand(hot):
        e = lax.dot_general(left, hot, NN, preferred_element_type=F32)
        return e[:dirs] + e[dirs:2 * dirs] + e[2 * dirs:]

    squares = jnp.zeros((dirs, rows), F32)
    for i in range(S):
        within = proj[i] - expand(onehot[i])
        squares = squares + within * within
    within_q = jnp.sum(squares, axis=1, keepdims=True)
    quotients = between_q / within_q
    own = expand((classes == lab_ref[...]).astype(F32).astype(BF16))
    combined = ((own - grand) - quotients * (proj[s] - own)).astype(BF16)
    scale = to_col(step_ref[...], dirs) / within_q
    quo_ref[...] = to_row(quotients, dirs)

    for r in list(range(1, S)) + [0]:
        t = lax.rem(s + r, S)
        for k in range(nch):
            span = pl.ds(pl.multiple_of(t * piece + k * ch, BLOCK), ch)
            g = jnp.dot(combined, mv[:, span], preferred_element_type=F32)
            if r == 0:
                grecv[s, k] = g
            else:
                gsend[r - 1, k] = g
                start(remote(
                    gsend.at[r - 1, k], grecv.at[s, k], g_send.at[r, k], g_recv.at[s, k], (t, c)
                ))
    total = jnp.zeros((dirs, ch), F32)
    for k in range(nch):
        for r in range(1, S):
            t = lax.rem(s + r, S)
            remote(
                gsend.at[r - 1, k], grecv.at[t, k], g_send.at[r, k], g_recv.at[t, k], (s, c)
            ).wait_recv()
        g = functools.reduce(jnp.add, [grecv[i, k] for i in range(S)])
        span = pl.ds(pl.multiple_of(s * piece + k * ch, BLOCK), ch)
        kept = (dv[:, span].astype(F32) + scale * g) * mask[k]
        fbuf[s, k] = kept
        total = total + kept * kept
    sbuf[me] = to_row(jnp.sum(total, axis=1, keepdims=True), BLOCK)

    def tell(r, carry):
        t = lax.rem(me + r, N)
        remote(
            sbuf.at[me], sbuf.at[me], s_send, s_recv, (lax.div(t, C), lax.rem(t, C))
        ).start()
        return carry

    if N <= 64:
        for r in range(1, N):
            tell(r, 0)
    else:
        lax.fori_loop(1, N, tell, 0)
    for r in range(1, S):
        t = lax.rem(s + r, S)
        start(remote(fbuf.at[s], fbuf.at[s], f_send.at[r], f_recv.at[s], (t, c)))
    out_copies = [pltpu.make_async_copy(fbuf.at[s], kept_hbm.at[s], o_sem.at[0])]
    out_copies[0].start()
    others = sbuf.at[pl.ds(0, N - 1)]
    for r in range(1, S):
        t = lax.rem(s + r, S)
        remote(fbuf.at[t], fbuf.at[t], f_send.at[r], f_recv.at[t], (s, c)).wait_recv()
        copy = pltpu.make_async_copy(fbuf.at[t], kept_hbm.at[t], o_sem.at[r])
        copy.start()
        out_copies.append(copy)
    pltpu.make_async_copy(others, others, s_recv).wait()
    sums = to_col(jnp.sum(sbuf[...], axis=0), dirs)
    norm = lax.rsqrt(sums / (sup_ref.shape[1] * BLOCK) + STABILITY_FLOOR)
    norm_ref[...] = jnp.broadcast_to(norm, (dirs, BLOCK))
    for copy in sent:
        copy.wait_send()
    pltpu.make_async_copy(others, others, s_send).wait()
    for copy in out_copies:
        copy.wait()


def finish(S, nch, ch, kept_ref, norm_ref, quo_in, out_ref, quo_ref):
    norm = norm_ref[:, :1]
    for i in range(S):
        for k in range(nch):
            at = (i * nch + k) * ch
            out_ref[:, at:at + ch] = kept_ref[i, k] * norm
    quo_ref[...] = quo_in[...]


def per_device(S, C, methylation, labels, directions, step_sizes, supports):
    rows, cols = methylation.shape
    dirs = directions.shape[0]
    A = 1
    B, N, G, R = C // A, S * C, S * A, dirs // A
    piece = cols // S
    nk = divisor(cols // BLOCK, 7)
    nch = divisor(piece // BLOCK, 4)
    ch = piece // nch
    dma = pltpu.SemaphoreType.DMA
    vmem = pl.BlockSpec(memory_space=pltpu.VMEM)
    hbm = pl.BlockSpec(memory_space=pltpu.HBM)
    kept, norm, quotients = pl.pallas_call(
        functools.partial(kernel, S, C, A, nk, nch),
        out_shape=(
            jax.ShapeDtypeStruct((S, nch, dirs, ch), F32),
            jax.ShapeDtypeStruct((dirs, BLOCK), F32),
            jax.ShapeDtypeStruct((1, dirs), F32),
        ),
        in_specs=[hbm, hbm, vmem, vmem, vmem],
        out_specs=(hbm, vmem, vmem),
        scratch_shapes=[
            pltpu.VMEM((rows, cols), BF16),
            pltpu.VMEM((dirs, cols), BF16),
            pltpu.VMEM((A, R, rows), F32),
            pltpu.VMEM((A, R, rows), F32),
            pltpu.VMEM((B, R, rows), F32),
            pltpu.VMEM((G, R, rows), F32),
            pltpu.VMEM((S, dirs, rows), F32),
            pltpu.VMEM((S, 1, rows), jnp.int32),
            pltpu.VMEM((max(S - 1, 1), nch, dirs, ch), F32),
            pltpu.VMEM((S, nch, dirs, ch), F32),
            pltpu.VMEM((S, nch, dirs, ch), F32),
            pltpu.VMEM((N, 1, BLOCK), F32),
            pltpu.VMEM((nch, dirs, ch), F32),
            dma((nk,)), dma, dma((S,)), dma((S,)), dma((A,)), dma((A,)), dma((B,)), dma((B,)),
            dma((G,)), dma((G,)), dma((S, nch)), dma((S, nch)), dma((S,)), dma((S,)), dma, dma,
            dma((S,)),
        ],
        compiler_params=pltpu.CompilerParams(
            collective_id=0, has_side_effects=True, vmem_limit_bytes=67_000_000
        ),
        name="flow_step",
    )(methylation, directions, labels.reshape(1, rows), step_sizes.reshape(1, dirs), supports)
    out, quotients = pl.pallas_call(
        functools.partial(finish, S, nch, ch),
        out_shape=(
            jax.ShapeDtypeStruct((dirs, cols), F32),
            jax.ShapeDtypeStruct((1, dirs), F32),
        ),
        in_specs=[vmem, vmem, vmem],
        out_specs=(vmem, vmem),
        compiler_params=pltpu.CompilerParams(vmem_limit_bytes=67_000_000),
        name="finish",
    )(kept, norm, quotients)
    return out, quotients.reshape(dirs)


def solution(mesh):
    in_specs = (P("samp", "cpg"), P("samp"), P(None, "cpg"), P(), P())
    out_specs = (P(None, "cpg"), P())
    return jax.shard_map(
        functools.partial(per_device, mesh.shape["samp"], mesh.shape["cpg"]),
        mesh=mesh, in_specs=in_specs, out_specs=out_specs, check_vma=False,
    )
```
